128 devices in a mesh: arc: 4 (over z), nr: 8 (over y_lo, x), nc: 4 (over y_hi, core).
Axes of the slice: x: 4, y: 4 (y_hi: 2, y_lo: 2; y = y_hi * 2 + y_lo), z: 4, core: 2. Of those that a mesh axis runs over, the one named last changes fastest.
Arguments:
- design: float32 [2048, 16384], P('arc', ('nr', 'nc')), may hold values from -6 to 6
- root_tiles: float32 [4, 512, 512], P('arc'), may hold values from -0.25 to 0.25
- row_weights: float32 [2048], P('arc'), may hold values from 0.25 to 4
- prior_sd: float32 [16384], P(('nr', 'nc')), may hold values from 0.1 to 1
- probe_signs: int32 [16384, 128], P(('nr', 'nc')), may hold values from -1 to 1, as said below
Outputs:
- normals: float32 [8, 2048, 8, 2048], P('nr', 'arc', None, 'nc')
- probe_products: float32 [8, 2048, 128], P('nr', ('arc', 'nc'))
- design_probe: float32 [2048, 128], P(('arc', 'nr', 'nc'))
The draws below stay inside these ranges and needn't reach their ends.
Inputs may be any that keep to these rules, and one draw needn't show every extreme that they name: `probe_signs`: every entry is -1 or 1.
All inputs are finite; a program needn't handle non-finite values.
Results may differ from the reference program's by a relative error of at most 0.000073.
Values sent between devices are 32-bit elements; how exact they have to be, the bound alone decides.
No kernel may reach another device: no remote copies, remote signals or barrier semaphores. Data moves between devices by JAX's collectives and lax.ppermute only.
A program may use at most 128 MiB of HBM per device.

```python
import math
import jax
import jax.numpy as jnp
from jax import lax

P_SIZE = 16384
PROBES = 128
BLK = 512
ROWS = 2048
NBLK = 4
N_NR = 8


def draw_probe_signs(key, part):
    return (jax.random.randint(key, (P_SIZE, PROBES), 0, 2) * 2 - 1).astype(jnp.int32)


def steps_of(own_key, shape, shards, low, top_value):
    def one(dim, blocks):
        steps = jax.random.uniform(jax.random.fold_in(jax.random.fold_in(own_key, 6), dim), (blocks,), jnp.float32, low / len(shards), top_value / len(shards))
        return jnp.repeat(jnp.exp(steps), shape[dim] // blocks).reshape((-1,) + (1,) * (len(shape) - dim - 1))

    level = one(*shards[0])
    for cut in shards[1:]:
        level = level * one(*cut)
    return level


def bell_draw(key, shape, scale, bound, pieces=(), held_as=jnp.bfloat16):
    values = jax.random.normal(key, shape, jnp.float32) * scale
    if len(pieces) > 0:
        values = steps_of(key, shape, pieces, -0.22, 0.18) * values
    return jnp.clip(values, min=-bound, max=bound).astype(held_as)


def setup_inputs(seed: int = 0) -> dict:
    key_of = jax.random.split(jax.random.key(seed), 6)
    return {
        "design": bell_draw(key_of[0], (ROWS, P_SIZE), 1.0, 6.0, ((0, 4), (1, 32)), jnp.float32),
        "root_tiles": bell_draw(key_of[1], (NBLK, BLK, BLK), BLK ** -0.5, 0.25, ((0, 4),), jnp.float32),
        "row_weights": jnp.clip(jnp.exp(math.log(4.0) - 2.7725887 * jax.random.uniform(key_of[2], (ROWS,), jnp.float32) ** steps_of(key_of[2], (ROWS,), ((0, 4),), -0.2, 0.2)), 0.25, 4.0),
        "prior_sd": jnp.clip(jnp.exp(math.log(1.0) - 2.3025851 * jax.random.uniform(key_of[3], (P_SIZE,), jnp.float32) ** steps_of(key_of[3], (P_SIZE,), ((0, 32),), -0.2, 0.2)), 0.1, 1.0),
        "probe_signs": draw_probe_signs(jax.random.fold_in(key_of[5], 71), 0),
    }


def reference(design, root_tiles, row_weights, prior_sd, probe_signs):
    tile_count, tile_size, _ = root_tiles.shape
    param_width = design.shape[1]
    blocks = design.reshape(tile_count, tile_size, param_width)
    whitened = jnp.einsum('bij,bjk->bik', root_tiles, blocks, precision=lax.Precision.HIGHEST).reshape(-1, param_width)
    scaled = whitened * (row_weights / ROWS)[:, None]
    gram_matrix = jnp.dot(scaled.T, whitened, precision=lax.Precision.HIGHEST, preferred_element_type=jnp.float32)
    block_size = param_width // N_NR
    normals = gram_matrix.reshape(N_NR, block_size, N_NR, block_size)
    probes = probe_signs.astype(jnp.float32) * prior_sd[:, None]
    applied = jnp.dot(gram_matrix, probes, precision=lax.Precision.HIGHEST, preferred_element_type=jnp.float32)
    design_probe = jnp.dot(whitened, applied, precision=lax.Precision.HIGHEST, preferred_element_type=jnp.float32) * (P_SIZE ** -0.5)
    return normals, applied.reshape(N_NR, block_size, PROBES), design_probe
```

```python
import jax
import jax.numpy as jnp
from jax import lax
from jax.experimental import pallas as pl
from jax.experimental.pallas import tpu as pltpu
from jax.sharding import Mesh, PartitionSpec as P

P_SIZE = 16384
ROWS = 2048
TILE = 512
F32 = jnp.float32
BF16 = jnp.bfloat16


def split(x):
    hi = x.astype(BF16)
    lo = (x - hi.astype(F32)).astype(BF16)
    return hi, lo


def dot(a, b):
    return jnp.dot(a, b, preferred_element_type=F32)


def dot3(a, b):
    ah, al = a
    bh, bl = b
    return dot(ah, bh) + (dot(ah, bl) + dot(al, bh))


def whiten_kernel(design_ref, root_ref, weight_ref, sd_ref, sign_ref, w_ref, st_ref, u_ref):
    w = dot3(split(root_ref[0]), split(design_ref[...]))
    w_ref[...] = w
    st_ref[...] = w.T * (weight_ref[...] * (1.0 / ROWS))
    wh, wl = split(w * sd_ref[...])
    signs = sign_ref[...].astype(F32).astype(BF16)
    u_ref[...] = dot(wh, signs) + dot(wl, signs)


def whiten(design, root, weights, sd, signs):
    return pl.pallas_call(
        whiten_kernel,
        out_shape=(
            jax.ShapeDtypeStruct((TILE, TILE), F32),
            jax.ShapeDtypeStruct((TILE, TILE), F32),
            jax.ShapeDtypeStruct((TILE, 128), F32),
        ),
        name="whiten",
    )(design, root, weights.reshape(1, TILE), sd.reshape(1, TILE), signs)


def gram_first_kernel(where_ref, t0, t1, t2, t3, a_ref, g_ref, hi_ref, lo_ref, acc):
    col, j = pl.program_id(0), pl.program_id(1)

    @pl.when(col == 0)
    def _():
        for i, t in enumerate((t0, t1, t2, t3)):

            @pl.when(j == i)
            def _():
                hi, lo = split(t[...])
                hi_ref[i] = hi
                lo_ref[i] = lo

    part = dot3((hi_ref[j], lo_ref[j]), split(a_ref[0, 0]))

    @pl.when(j == 0)
    def _():
        acc[...] = part

    @pl.when(j > 0)
    def _():
        acc[...] += part

    @pl.when(j == 3)
    def _():
        g_ref[0] = acc[...]


def gram_first(where, parts, gathered):
    whole = pl.BlockSpec((TILE, TILE), lambda i, j, w: (0, 0))
    kept = pl.BlockSpec((4, TILE, TILE), lambda i, j, w: (0, 0, 0))
    return pl.pallas_call(
        gram_first_kernel,
        grid_spec=pltpu.PrefetchScalarGridSpec(
            num_scalar_prefetch=1,
            grid=(4, 4),
            in_specs=[whole] * 4
            + [pl.BlockSpec((1, 1, TILE, TILE), lambda i, j, w: (w[0] ^ j, i, 0, 0))],
            out_specs=(
                pl.BlockSpec((1, TILE, TILE), lambda i, j, w: (i, 0, 0)),
                kept,
                kept,
            ),
            scratch_shapes=[pltpu.VMEM((TILE, TILE), F32)],
        ),
        out_shape=(
            jax.ShapeDtypeStruct((4, TILE, TILE), F32),
            jax.ShapeDtypeStruct((4, TILE, TILE), BF16),
            jax.ShapeDtypeStruct((4, TILE, TILE), BF16),
        ),
        compiler_params=pltpu.CompilerParams(vmem_limit_bytes=56 << 20),
        name="gram_first",
    )(where, *parts, gathered)


def gram_last_kernel(where_ref, hi_ref, lo_ref, first_ref, a_ref, out_ref, acc, held, sems):
    col, j = pl.program_id(0), pl.program_id(1)
    part = dot3((hi_ref[j], lo_ref[j]), split(a_ref[0, 0]))

    @pl.when(j == 0)
    def _():
        acc[...] = part

    @pl.when(j > 0)
    def _():
        acc[...] += part

    own = where_ref[1] * 4 + col
    other = (1 - where_ref[1]) * 4 + col

    @pl.when(j == 0)
    def _():
        for l in range(4):
            lanes = pl.ds(l * 128, 128)
            held[l, pl.ds(own, TILE, stride=8), :] = first_ref[0, :, lanes]

    @pl.when(j == 3)
    def _():
        for l in range(4):
            lanes = pl.ds(l * 128, 128)
            held[l, pl.ds(other, TILE, stride=8), :] = acc[:, lanes]

    @pl.when((j == 3) & (col == 3))
    def _():
        copies = [
            pltpu.make_async_copy(held.at[l], out_ref.at[:, pl.ds(l * 128, 128)], sems.at[l])
            for l in range(4)
        ]
        for copy in copies:
            copy.start()
        for copy in copies:
            copy.wait()


def gram_last(where, hi, lo, first, gathered):
    kept = pl.BlockSpec((4, TILE, TILE), lambda i, j, w: (0, 0, 0))
    return pl.pallas_call(
        gram_last_kernel,
        grid_spec=pltpu.PrefetchScalarGridSpec(
            num_scalar_prefetch=1,
            grid=(4, 4),
            in_specs=[
                kept,
                kept,
                pl.BlockSpec((1, TILE, TILE), lambda i, j, w: (i, 0, 0)),
                pl.BlockSpec((1, 1, TILE, TILE), lambda i, j, w: (w[0] ^ j, i, 0, 0)),
            ],
            out_specs=pl.BlockSpec(memory_space=pl.ANY),
            scratch_shapes=[
                pltpu.VMEM((TILE, TILE), F32),
                pltpu.VMEM((4, TILE * 8, 128), F32),
                pltpu.SemaphoreType.DMA((4,)),
            ],
        ),
        out_shape=jax.ShapeDtypeStruct((TILE * 8, TILE), F32),
        compiler_params=pltpu.CompilerParams(vmem_limit_bytes=56 << 20),
        name="gram_last",
    )(where, hi, lo, first, gathered)


def swap(x, axis, size=2, bit=1):
    return lax.ppermute(x, axis, [(i, i ^ bit) for i in range(size)])


def transpose_devices(x):
    return lax.ppermute(
        x, ("z", "yh", "k"), [(z * 4 + c, c * 4 + z) for z in range(4) for c in range(4)]
    )


def halve(x, axis, size=2, bit=1):
    mine = (lax.axis_index(axis) // bit) % 2
    half = x.shape[0] // 2
    keep = lax.dynamic_slice_in_dim(x, mine * half, half, 0)
    send = lax.dynamic_slice_in_dim(x, (1 - mine) * half, half, 0)
    return keep + swap(send, axis, size, bit)


def probe_chain(w, st, u):
    for axis, size, bit in (("k", 2, 1), ("yh", 2, 1), ("yl", 2, 1), ("x", 4, 1), ("x", 4, 2)):
        u = u + swap(u, axis, size, bit)
    applied = jnp.dot(st, u, precision=lax.Precision.HIGH, preferred_element_type=F32)
    for bit in (1, 2):
        applied = applied + swap(applied, "z", 4, bit)
    piece = lax.dynamic_slice_in_dim(applied, lax.axis_index("z") * 128, 128, 0)
    products = transpose_devices(piece)
    share = jnp.dot(w, applied, precision=lax.Precision.HIGH, preferred_element_type=F32)
    share = share * P_SIZE ** (-0.5)
    for axis, size, bit in (("yl", 2, 1), ("x", 4, 2), ("x", 4, 1), ("yh", 2, 1), ("k", 2, 1)):
        share = halve(share, axis, size, bit)
    return products, share


def per_device(design, root_tiles, row_weights, prior_sd, probe_signs):
    where = jnp.stack([lax.axis_index("yh") * 2 + lax.axis_index("k"), lax.axis_index("yl")])
    where = where.astype(jnp.int32)
    w, st, u = whiten(design, root_tiles, row_weights, prior_sd, probe_signs)
    own = lax.all_gather(w, ("z", "x"), axis=0, tiled=True)
    other = lax.all_gather(swap(w, "yl"), ("z", "x"), axis=0, tiled=True)
    t0 = transpose_devices(st)
    t2 = swap(t0, "yh")
    t1 = swap(t0, "k")
    t3 = swap(t2, "k")
    first, hi, lo = gram_first(where, (t0, t1, t2, t3), own.reshape(4, 4, TILE, TILE))
    normals = gram_last(where, hi, lo, first, other.reshape(4, 4, TILE, TILE))
    products, share = probe_chain(w, st, u)
    return normals.reshape(1, TILE, 8, TILE), products[None], share


def solution(mesh):
    split_mesh = Mesh(mesh.devices.reshape(4, 2, 4, 2, 2), ("z", "yl", "x", "yh", "k"))
    nr, nc = ("yl", "x"), ("yh", "k")
    in_specs = (
        P("z", nr + nc),
        P("z", None, None),
        P("z"),
        P(nr + nc),
        P(nr + nc, None),
    )
    out_specs = (
        P(nr, "z", None, nc),
        P(nr, ("z",) + nc, None),
        P(("z",) + nr + nc, None),
    )
    return jax.shard_map(
        per_device, mesh=split_mesh, in_specs=in_specs, out_specs=out_specs, check_vma=False
    )
```
